32 devices in a mesh: section: 2 (over x), tensor: 2 (over core), dp: 8 (over z, y).
Axes of the slice: x: 2, y: 2, z: 4, core: 2. Of those that a mesh axis runs over, the one named last changes fastest.
Arguments:
- images: bfloat16 [6304, 768], P('dp'), may hold values from -40 to 40
- cotangent: bfloat16 [6304, 768], P('dp'), may hold values from -6 to 6
- live_images: int32 [8], P('dp'), may hold values from 3 to 4, as said below
- attn_norm_gain: float32 [2, 768], P('section'), may hold values from 0.5 to 1.5
- attn_norm_bias: float32 [2, 768], P('section'), may hold values from -3 to 3
- qkv_weight: bfloat16 [2, 3, 768, 768], P('section', None, None, 'tensor'), may hold values from -7 to 7
- qv_bias: float32 [2, 2, 768], P('section', None, 'tensor'), may hold values from -3 to 3
- out_weight: bfloat16 [2, 768, 768], P('section', 'tensor'), may hold values from -0.875 to 0.875
- out_bias: float32 [2, 768], P('section'), may hold values from -3 to 3
- mlp_norm_gain: float32 [2, 768], P('section'), may hold values from 0.5 to 1.5
- mlp_norm_bias: float32 [2, 768], P('section'), may hold values from -3 to 3
- up_weight: bfloat16 [2, 768, 3072], P('section', None, 'tensor'), may hold values from -0.21875 to 0.21875
- up_bias: float32 [2, 3072], P('section', 'tensor'), may hold values from -3 to 3
- down_weight: bfloat16 [2, 3072, 768], P('section', 'tensor'), may hold values from -0.109375 to 0.109375
- down_bias: float32 [2, 768], P('section'), may hold values from -3 to 3
Outputs:
- section_out: bfloat16 [2, 6304, 768], P('section', 'dp')
- input_grad: bfloat16 [2, 6304, 768], P('section', 'dp')
- grad_attn_norm_gain: float32 [2, 768], P('section', 'dp')
- grad_attn_norm_bias: float32 [2, 768], P('section', 'dp')
- grad_qkv_weight: float32 [2, 3, 768, 768], P('section', None, 'dp', 'tensor')
- grad_qv_bias: float32 [2, 2, 768], P('section', None, ('tensor', 'dp'))
- grad_out_weight: float32 [2, 768, 768], P('section', 'tensor', 'dp')
- grad_out_bias: float32 [2, 768], P('section', 'dp')
- grad_mlp_norm_gain: float32 [2, 768], P('section', 'dp')
- grad_mlp_norm_bias: float32 [2, 768], P('section', 'dp')
- grad_up_weight: float32 [2, 768, 3072], P('section', 'dp', 'tensor')
- grad_up_bias: float32 [2, 3072], P('section', ('tensor', 'dp'))
- grad_down_weight: float32 [2, 3072, 768], P('section', 'tensor', 'dp')
- grad_down_bias: float32 [2, 768], P('section', 'dp')
The draws below stay inside these ranges and needn't reach their ends.
Inputs may be any that keep to these rules, and one draw needn't show every extreme that they name: `live_images`: each replica has 3 or 4 live images, in its first slots; both counts occur.
All inputs are finite; a program needn't handle non-finite values.
Results may differ from the reference program's by a relative error of at most 0.019.
Values may be sent and summed in bfloat16 or wider, within the bound.
No kernel may reach another device: no remote copies, remote signals or barrier semaphores. Data moves between devices by JAX's collectives and lax.ppermute only.
A program may use at most 192 MiB of HBM per device.

```python
import math
from functools import partial
import jax
import jax.numpy as jnp
from jax import lax

D = 768
HEAD_DIM = 64
FF = 3072
SEQ = 197
SLOTS = 4
TOKENS = 6304
N_SECTION = 2
N_DP = 8


def draw_images(key, part):
    key_rows, key_cols, key_base = jax.random.split(key, 3)
    row_scale = jnp.exp(jax.random.uniform(key_rows, (TOKENS, 1), minval=math.log(0.3), maxval=math.log(3.0)))
    col_scale = jnp.exp(jax.random.uniform(key_cols, (1, D), minval=-0.5, maxval=0.5))
    base_values = jnp.clip(jax.random.normal(key_base, (TOKENS, D)), -6.0, 6.0)
    return jnp.clip(base_values * row_scale * col_scale, -40.0, 40.0).astype(jnp.bfloat16)


def draw_qkv_weight(key, part):
    key_base = jax.random.fold_in(key, 0)
    base_values = jnp.clip(jax.random.normal(key_base, (N_SECTION, 3, D, D)), -6.0, 6.0) * D ** (-0.5)
    return jnp.clip(base_values, -7.0, 7.0).astype(jnp.bfloat16)


def draw_live_images(key, part):
    key_base, key_order = jax.random.split(key, 2)
    counts = SLOTS - 1 + jax.random.randint(key_base, (N_DP,), 0, 2)
    order = jax.random.permutation(key_order, N_DP)
    counts = counts.at[order[0]].set(SLOTS).at[order[1]].set(SLOTS - 1)
    return counts.astype(jnp.int32)


def with_spikes(result, key, source, target, parts, factor):
    owner, partner = [(jnp.arange(result.shape[axis_at]) // (result.shape[axis_at] // parts)).reshape([-1 if axis == axis_at else 1 for axis in range(result.ndim)]) for axis_at in (source, target)]
    chosen = jax.random.permutation(key, parts)[partner]
    strong = (owner == chosen) | (owner == (partner + parts // 2) % parts)
    return jnp.where(strong, factor * result, result)


def shard_levels(key, extent, pieces, smallest, largest):
    level, own = 1.0, jax.random.fold_in(key, 6)
    for dim, shards_of in pieces:
        draws = jnp.exp(jax.random.uniform(jax.random.fold_in(own, dim), (shards_of,), jnp.float32, smallest / len(pieces), largest / len(pieces)))
        level = level * jnp.repeat(draws, extent[dim] // shards_of).reshape([-1 if axis == dim else 1 for axis in range(len(extent))])
    return level


def noise(stream_key, extent, deviation, most, pieces=(), kind=jnp.bfloat16):
    array = jax.random.normal(stream_key, extent, jnp.float32) * deviation
    if len(pieces) > 0:
        array = shard_levels(stream_key, extent, pieces, -0.22, 0.18) * array
    return jnp.clip(array, min=-most, max=most).astype(kind)


def noise_with(rng, shape, deviation, limit, shards, heavy, kind=jnp.bfloat16):
    array = deviation * jax.random.normal(rng, shape, jnp.float32)
    if shards:
        array = array * shard_levels(rng, shape, shards, -0.22, 0.18)
    return jnp.clip(with_spikes(array, jax.random.fold_in(rng, 3), *heavy), -limit, limit).astype(kind)


def setup_inputs(seed: int = 0) -> dict:
    arg_keys = jax.random.split(jax.random.key(seed), 16)
    return {
        "images": draw_images(jax.random.fold_in(arg_keys[15], 71), 0),
        "cotangent": noise_with(arg_keys[1], (TOKENS, D), 1.0, 6.0, ((0, 8),), (0, 1, 8, 2.0)),
        "live_images": draw_live_images(jax.random.fold_in(arg_keys[15], 71), 0),
        "attn_norm_gain": jnp.clip(1.0 + 0.1 * jax.random.normal(arg_keys[3], (N_SECTION, D), jnp.float32), 0.5, 1.5),
        "attn_norm_bias": noise(arg_keys[4], (N_SECTION, D), 0.5, 3.0, ((0, 2),), jnp.float32),
        "qkv_weight": draw_qkv_weight(jax.random.fold_in(arg_keys[15], 71), 0),
        "qv_bias": noise(arg_keys[6], (N_SECTION, 2, D), 0.5, 3.0, ((0, 2), (2, 2)), jnp.float32),
        "out_weight": noise(arg_keys[7], (N_SECTION, D, D), (D // 16) ** -0.5, 0.875, ((0, 2), (1, 2))),
        "out_bias": noise(arg_keys[8], (N_SECTION, D), 0.5, 3.0, ((0, 2),), jnp.float32),
        "mlp_norm_gain": jnp.clip(1.0 + 0.1 * jax.random.normal(arg_keys[9], (N_SECTION, D), jnp.float32), 0.5, 1.5),
        "mlp_norm_bias": noise(arg_keys[10], (N_SECTION, D), 0.5, 3.0, ((0, 2),), jnp.float32),
        "up_weight": noise(arg_keys[11], (N_SECTION, D, FF), D ** -0.5, 0.21875, ((0, 2), (2, 2))),
        "up_bias": noise(arg_keys[12], (N_SECTION, FF), 0.5, 3.0, ((0, 2), (1, 2)), jnp.float32),
        "down_weight": noise(arg_keys[13], (N_SECTION, FF, D), FF ** -0.5, 0.109375, ((0, 2), (1, 2))),
        "down_bias": noise(arg_keys[14], (N_SECTION, D), 0.5, 3.0, ((0, 2),), jnp.float32),
    }


EPS = 1e-06

def normalize(rows_in, ln_gain, ln_shift):
    average = lax.optimization_barrier(jnp.mean(rows_in, axis=-1, keepdims=True))
    centred = rows_in - average
    variance = lax.optimization_barrier(jnp.mean(centred * centred, axis=-1, keepdims=True))
    inverse = lax.rsqrt(variance + EPS)
    standard = centred * inverse
    return (standard, inverse, (standard * ln_gain + ln_shift).astype(jnp.bfloat16))

def normalize_back(grad_normed, standard, inverse, ln_gain):
    scaled = grad_normed * ln_gain
    inner = lax.optimization_barrier(jnp.mean(scaled, axis=-1, keepdims=True)) + standard * lax.optimization_barrier(jnp.mean(scaled * standard, axis=-1, keepdims=True))
    return (inverse * (scaled - inner), lax.optimization_barrier(jnp.sum(grad_normed * standard, axis=0)), lax.optimization_barrier(jnp.sum(grad_normed, axis=0)))

def matmul(left, right):
    return jnp.dot(left, right, preferred_element_type=jnp.float32)

def outer_rows(left, right):
    return lax.dot_general(left, right, (((0,), (0,)), ((), ())), preferred_element_type=jnp.float32)

def product(form, left, right):
    return jnp.einsum(form, left.astype(jnp.float32), right.astype(jnp.float32), precision=lax.Precision.HIGHEST)

def by_heads(matrix):
    row_count, col_count = matrix.shape
    return matrix.reshape(row_count // SEQ, SEQ, col_count // HEAD_DIM, HEAD_DIM)

def by_rows(tensor):
    image_count, seq_count, head_count, head_width = tensor.shape
    return tensor.reshape(image_count * seq_count, head_count * head_width)

def layer_forward(layer_weights, entering, token_mask, branch_total):
    gain_in, shift_in, qkv_weight, qv_bias, out_weight, out_bias, gain_mid, shift_mid, up_weight, up_bias, down_weight, down_bias = layer_weights
    standard_in, inverse_in, normed_in = normalize(entering.astype(jnp.float32), gain_in, shift_in)
    queries = (matmul(normed_in, qkv_weight[0]) + qv_bias[0]).astype(jnp.bfloat16)
    key_rows = matmul(normed_in, qkv_weight[1]).astype(jnp.bfloat16)
    values = (matmul(normed_in, qkv_weight[2]) + qv_bias[1]).astype(jnp.bfloat16)
    scores = product('bqhd,bkhd->bhqk', by_heads(queries), by_heads(key_rows)) * 0.125
    log_totals = jax.nn.logsumexp(scores, axis=-1)
    probs_b = jnp.exp(scores - log_totals[..., None]).astype(jnp.bfloat16)
    context = by_rows(product('bhqk,bkhd->bqhd', probs_b, by_heads(values))).astype(jnp.bfloat16)
    residual = entering.astype(jnp.float32) + branch_total(matmul(context, out_weight)) + out_bias
    standard_mid, inverse_mid, normed_mid = normalize(residual, gain_mid, shift_mid)
    up_act = matmul(normed_mid, up_weight) + up_bias
    active = jax.nn.gelu(up_act, approximate=False).astype(jnp.bfloat16)
    leaving = ((residual + branch_total(matmul(active, down_weight)) + down_bias) * token_mask).astype(jnp.bfloat16)
    return (leaving, (normed_in, queries, key_rows, values, log_totals, context, residual, normed_mid, up_act, active))

def layer_backward(layer_weights, entering, stored, arriving, token_mask, input_total):
    gain_in, shift_in, qkv_weight, qv_bias, out_weight, out_bias, gain_mid, shift_mid, up_weight, up_bias, down_weight, down_bias = layer_weights
    normed_in, queries, key_rows, values, log_totals, context, residual, normed_mid, up_act, active = stored
    grad_out = arriving.astype(jnp.float32) * token_mask
    grad_out_b = grad_out.astype(jnp.bfloat16)
    grad_active = matmul(grad_out_b, down_weight.T)
    unused, pullback = jax.vjp(partial(jax.nn.gelu, approximate=False), up_act)
    grad_up = pullback(grad_active)[0].astype(jnp.bfloat16)
    grad_mid = input_total(matmul(grad_up, up_weight.T))
    standard_mid, inverse_mid, unused_mid = normalize(residual, gain_mid, shift_mid)
    back_mid, grad_gain_mid, grad_shift_mid = normalize_back(grad_mid, standard_mid, inverse_mid, gain_mid)
    grad_residual = grad_out + back_mid
    grad_residual_b = grad_residual.astype(jnp.bfloat16)
    grad_context = matmul(grad_residual_b, out_weight.T).astype(jnp.bfloat16)
    scores = product('bqhd,bkhd->bhqk', by_heads(queries), by_heads(key_rows)) * 0.125
    attn_probs = jnp.exp(scores - log_totals[..., None])
    probs_b = attn_probs.astype(jnp.bfloat16)
    grad_probs = product('bqhd,bkhd->bhqk', by_heads(grad_context), by_heads(values))
    grad_scores = (attn_probs * (grad_probs - lax.optimization_barrier(jnp.sum(attn_probs * grad_probs, axis=-1, keepdims=True))) * 0.125).astype(jnp.bfloat16)
    grad_queries = by_rows(product('bhqk,bkhd->bqhd', grad_scores, by_heads(key_rows))).astype(jnp.bfloat16)
    grad_keys = by_rows(product('bhqk,bqhd->bkhd', grad_scores, by_heads(queries))).astype(jnp.bfloat16)
    grad_values = by_rows(product('bhqk,bqhd->bkhd', probs_b, by_heads(grad_context))).astype(jnp.bfloat16)
    grad_in = input_total(matmul(grad_queries, qkv_weight[0].T) + matmul(grad_keys, qkv_weight[1].T) + matmul(grad_values, qkv_weight[2].T))
    standard_in, inverse_in, unused_in = normalize(entering.astype(jnp.float32), gain_in, shift_in)
    back_in, grad_gain_in, grad_shift_in = normalize_back(grad_in, standard_in, inverse_in, gain_in)
    leaving = (grad_residual + back_in).astype(jnp.bfloat16)
    small_terms = (grad_gain_in, grad_shift_in, lax.optimization_barrier(jnp.sum(grad_residual, axis=0)), grad_gain_mid, grad_shift_mid, lax.optimization_barrier(jnp.sum(grad_out, axis=0)))
    operands = (grad_out_b, grad_up, grad_residual_b, grad_queries, grad_keys, grad_values)
    return (leaving, small_terms, operands)

def weight_terms(stored, operands):
    normed_in, queries, key_rows, values, log_totals, context, residual, normed_mid, up_act, active = stored
    grad_out_b, grad_up, grad_residual_b, grad_queries, grad_keys, grad_values = operands
    mlp_terms = (outer_rows(normed_mid, grad_up), lax.optimization_barrier(jnp.sum(grad_up.astype(jnp.float32), axis=0)), outer_rows(active, grad_out_b))
    attn_terms = (jnp.stack([outer_rows(normed_in, grad_queries), outer_rows(normed_in, grad_keys), outer_rows(normed_in, grad_values)]), jnp.stack([lax.optimization_barrier(jnp.sum(grad_queries.astype(jnp.float32), axis=0)), lax.optimization_barrier(jnp.sum(grad_values.astype(jnp.float32), axis=0))]), outer_rows(context, grad_residual_b))
    return (mlp_terms, attn_terms)

def assemble(small_terms, mlp_terms, attn_terms):
    return (small_terms[0], small_terms[1], attn_terms[0], attn_terms[1], attn_terms[2], small_terms[2], small_terms[3], small_terms[4], mlp_terms[0], mlp_terms[1], mlp_terms[2], small_terms[5])

def unchanged(term):
    return term

def reference(images, cotangent, live_images, attn_norm_gain, attn_norm_bias, qkv_weight, qv_bias, out_weight, out_bias, mlp_norm_gain, mlp_norm_bias, up_weight, up_bias, down_weight, down_bias):
    weights = (attn_norm_gain, attn_norm_bias, qkv_weight, qv_bias, out_weight, out_bias, mlp_norm_gain, mlp_norm_bias, up_weight, up_bias, down_weight, down_bias)
    block_rows = SLOTS * SEQ
    slot_index = jnp.arange(SLOTS, dtype=jnp.int32)
    live_slots = (slot_index[None, :] < live_images[:, None]).astype(jnp.float32)
    token_mask = jnp.repeat(live_slots, SEQ, axis=1).reshape(N_DP, block_rows, 1)
    section_inputs = [images.reshape(N_DP, block_rows, D)]
    for section_index in range(N_SECTION):
        layer_weights = tuple((weight[section_index] for weight in weights))

        def forward_block(operand_pair, layer_weights=layer_weights):
            return layer_forward(layer_weights, operand_pair[0], operand_pair[1], unchanged)[0]
        section_inputs.append(lax.map(forward_block, (section_inputs[-1], token_mask)))
    arriving = cotangent.reshape(N_DP, block_rows, D)
    section_grads = [None] * N_SECTION
    input_grads = [None] * N_SECTION
    for section_index in reversed(range(N_SECTION)):
        layer_weights = tuple((weight[section_index] for weight in weights))

        def backward_block(summed, members, layer_weights=layer_weights):
            entering, grad_arriving, block_mask = members
            stored = layer_forward(layer_weights, entering, block_mask, unchanged)[1]
            leaving, small_terms, operands = layer_backward(layer_weights, entering, stored, grad_arriving, block_mask, unchanged)
            mlp_terms, attn_terms = weight_terms(stored, operands)
            summed = jax.tree.map(lambda before, added: before + added, summed, assemble(small_terms, mlp_terms, attn_terms))
            return (summed, leaving)
        initial = tuple((jnp.zeros(weight.shape[1:], jnp.float32) for weight in weights))
        summed, leaving = lax.scan(backward_block, initial, (section_inputs[section_index], arriving, token_mask))
        section_grads[section_index] = summed
        input_grads[section_index] = leaving
        arriving = leaving
    section_out = jnp.stack(section_inputs[1:]).reshape(N_SECTION, TOKENS, D)
    input_grad = jnp.stack(input_grads).reshape(N_SECTION, TOKENS, D)
    stacked = [jnp.stack([section_grads[section_index][member] for section_index in range(N_SECTION)]) for member in range(12)]
    return (section_out, input_grad, stacked[0], stacked[1], stacked[2], stacked[3], stacked[4], stacked[5], stacked[6], stacked[7], stacked[8], stacked[9], stacked[10], stacked[11])
```

```python
import functools

import jax
import jax.numpy as jnp
from jax import lax
from jax.experimental import pallas as pl
from jax.experimental.pallas import tpu as pltpu
from jax.sharding import PartitionSpec as P

HEAD_DIM = 64
SEQ = 197
ROWS = 208
EPS = 1e-06
PAIR = 2 * HEAD_DIM
F32 = jnp.float32
BF16 = jnp.bfloat16

VMEM = pl.BlockSpec(memory_space=pltpu.VMEM)
SMEM = pl.BlockSpec(memory_space=pltpu.SMEM)


def nn(left, right):
    return lax.dot_general(left, right, (((1,), (0,)), ((), ())), preferred_element_type=F32)


def nt(left, right):
    return lax.dot_general(left, right, (((1,), (1,)), ((), ())), preferred_element_type=F32)


def tn(left, right):
    return lax.dot_general(left, right, (((0,), (0,)), ((), ())), preferred_element_type=F32)


def standardize(rows_in):
    centred = rows_in - jnp.mean(rows_in, axis=-1, keepdims=True)
    inverse = lax.rsqrt(jnp.mean(centred * centred, axis=-1, keepdims=True) + EPS)
    return centred * inverse, inverse


def lnb(grad_normed, standard, inverse, gain):
    scaled = grad_normed * gain
    inner = jnp.mean(scaled, axis=-1, keepdims=True) + standard * jnp.mean(
        scaled * standard, axis=-1, keepdims=True
    )
    return inverse * (scaled - inner)


def col_sum(matrix):
    return jnp.sum(matrix, axis=0, keepdims=True)


def call(body, outs, name, n_smem, n_vmem, scratch=(), flops=0, nbytes=0):
    return pl.pallas_call(
        body,
        out_shape=[jax.ShapeDtypeStruct(shape, kind) for shape, kind in outs],
        in_specs=[SMEM] * n_smem + [VMEM] * n_vmem,
        out_specs=[VMEM] * len(outs),
        scratch_shapes=list(scratch),
        name=name,
        compiler_params=pltpu.CompilerParams(vmem_limit_bytes=60 << 20),
    )


def fwd_attn_body(
    flags, own_in, arrived, gain, shift, wqkv_a, wqkv_b, qvb_a, qvb_b, wo_a, wo_b, ob,
    resid, entered, pack, ctx_own, qkv_s, probs_s,
):
    width = wo_a.shape[0]
    x = jnp.where(flags[0] == 0, own_in[...].astype(F32), arrived[...].astype(F32))
    entered[...] = x.astype(BF16)
    standard, unused = standardize(x)
    normed = (standard * gain[...] + shift[...]).astype(BF16)
    model = normed.shape[1]
    pack[:, 0:model] = normed
    total = x + ob[...]
    low = lax.broadcasted_iota(jnp.int32, (ROWS, PAIR), 1) < HEAD_DIM
    live_key = lax.broadcasted_iota(jnp.int32, (ROWS, ROWS), 1) < SEQ
    for half, (wqkv, qvb, wo) in enumerate(((wqkv_a, qvb_a, wo_a), (wqkv_b, qvb_b, wo_b))):
        for part in range(3):
            value = nn(normed, wqkv[part])
            if part != 1:
                value = value + qvb[part // 2 : part // 2 + 1]
            qkv_s[half, part] = value.astype(BF16)
        for pair in range(width // PAIR):
            cols = slice(pair * PAIR, (pair + 1) * PAIR)
            q2, k2, v2 = qkv_s[half, 0, :, cols], qkv_s[half, 1, :, cols], qkv_s[half, 2, :, cols]
            halves = []
            for side in range(2):
                mine = low if side == 0 else jnp.logical_not(low)
                q1 = jnp.where(mine, q2, jnp.zeros_like(q2))
                scores = jnp.where(live_key, nt(q1, k2) * 0.125, -1e30)
                powers = jnp.exp(scores - jnp.max(scores, axis=-1, keepdims=True))
                probs = (powers / jnp.sum(powers, axis=-1, keepdims=True)).astype(BF16)
                probs_s[half, 2 * pair + side] = probs
                halves.append(nn(probs, v2))
            ctx = jnp.where(low, halves[0], halves[1]).astype(BF16)
            if half == 0:
                ctx_own[:, cols] = ctx
            else:
                pack[:, model + pair * PAIR : model + (pair + 1) * PAIR] = ctx
        ctx_all = ctx_own[...] if half == 0 else pack[:, model : model + width]
        total = total + nn(ctx_all, wo[...])
    resid[...] = total


def fwd_mlp_body(
    mask, resid, gain, shift, up_a, up_b, ub_a, ub_b, down_a, down_b, db,
    leaving, pack, act_own, slope_s,
):
    hidden = up_a.shape[1]
    tile = 512 if hidden % 512 == 0 else hidden
    standard, unused = standardize(resid[...])
    normed = (standard * gain[...] + shift[...]).astype(BF16)
    model = normed.shape[1]
    pack[:, 0:model] = normed
    total = resid[...] + db[...]
    for half, (up, ub, down) in enumerate(((up_a, ub_a, down_a), (up_b, ub_b, down_b))):
        for at in range(0, hidden, tile):
            cols = slice(at, at + tile)
            u = nn(normed, up[:, cols]) + ub[:, cols]
            cdf = 0.5 + 0.5 * lax.erf(u * (0.5**0.5))
            active = (u * cdf).astype(BF16)
            slope_s[half, :, cols] = (
                cdf + u * (0.3989422804014327 * jnp.exp(-0.5 * (u * u)))
            ).astype(BF16)
            if half == 0:
                act_own[:, cols] = active
            else:
                pack[:, model + at : model + at + tile] = active
            total = total + nn(active, down[cols, :])
    leaving[...] = (total * mask[0]).astype(BF16)


def bwd_mlp_body(
    flags, mask, own_in, arrived, resid, slope_s, gain, up_a, up_b, down_a, down_b,
    grad_res, gout, pack, gup_own, small, bias,
):
    hidden = up_a.shape[1]
    tile = 512 if hidden % 512 == 0 else hidden
    last = flags[0] == flags[1] - 1
    grad_out = jnp.where(last, own_in[...].astype(F32), arrived[...].astype(F32)) * mask[0]
    grad_out_b = grad_out.astype(BF16)
    model = grad_out.shape[1]
    gout[...] = grad_out_b
    grad_mid = jnp.zeros(grad_out.shape, F32)
    for half, (up, down) in enumerate(((up_a, down_a), (up_b, down_b))):
        for at in range(0, hidden, tile):
            cols = slice(at, at + tile)
            grad_up = (slope_s[half, :, cols].astype(F32) * nt(grad_out_b, down[cols, :])).astype(BF16)
            if half == 0:
                gup_own[:, cols] = grad_up
            else:
                pack[:, model + at : model + at + tile] = grad_up
            bias[half : half + 1, cols] = col_sum(grad_up.astype(F32))
            grad_mid = grad_mid + nt(grad_up, up[:, cols])
    standard, inverse = standardize(resid[...])
    grad_residual = grad_out + lnb(grad_mid, standard, inverse, gain[...])
    grad_res[...] = grad_residual
    pack[:, 0:model] = grad_residual.astype(BF16)
    small[0:1] = col_sum(grad_residual)
    small[1:2] = col_sum(grad_mid * standard)
    small[2:3] = col_sum(grad_mid)
    small[3:4] = col_sum(grad_out)


def bwd_attn_body(
    grad_res, entered, qkv_s, probs_s, gain, wqkv_a, wqkv_b, wo_a, wo_b,
    leaving, gqkv_own, pack, small, bias,
):
    width = wo_a.shape[0]
    grad_residual = grad_res[...]
    grad_residual_b = grad_residual.astype(BF16)
    grad_in = jnp.zeros(grad_residual.shape, F32)
    low = lax.broadcasted_iota(jnp.int32, (ROWS, PAIR), 1) < HEAD_DIM
    for half, (wqkv, wo, kept) in enumerate(((wqkv_a, wo_a, gqkv_own), (wqkv_b, wo_b, pack))):
        grad_context = nt(grad_residual_b, wo[...]).astype(BF16)
        for pair in range(width // PAIR):
            cols = slice(pair * PAIR, (pair + 1) * PAIR)
            q2, k2, v2 = qkv_s[half, 0, :, cols], qkv_s[half, 1, :, cols], qkv_s[half, 2, :, cols]
            g2 = grad_context[:, cols]
            parts = []
            for side in range(2):
                mine = low if side == 0 else jnp.logical_not(low)
                g1 = jnp.where(mine, g2, jnp.zeros_like(g2))
                probs_b = probs_s[half, 2 * pair + side]
                probs = probs_b.astype(F32)
                grad_probs = nt(g1, v2)
                inner = jnp.sum(probs * grad_probs, axis=-1, keepdims=True)
                grad_scores = (probs * (grad_probs - inner) * 0.125).astype(BF16)
                parts.append((nn(grad_scores, k2), tn(grad_scores, q2), tn(probs_b, g2)))
            for part in range(3):
                merged = jnp.where(low, parts[0][part], parts[1][part]).astype(BF16)
                at = part * width + pair * PAIR
                kept[:, at : at + PAIR] = merged
                if part != 1:
                    bias[2 * half + part // 2 : 2 * half + part // 2 + 1, cols] = col_sum(
                        merged.astype(F32)
                    )
        for part in range(3):
            grad_in = grad_in + nt(kept[:, part * width : (part + 1) * width], wqkv[part])
    standard, inverse = standardize(entered[...].astype(F32))
    leaving[...] = (grad_residual + lnb(grad_in, standard, inverse, gain[...])).astype(BF16)
    small[0:1] = col_sum(grad_in * standard)
    small[1:2] = col_sum(grad_in)


def weight_body(n_dp, order, pieces, extra, spec, me_ref, *refs):
    n_in = len(spec)
    ins, tail, (sent, kept) = refs[:n_in], refs[n_in : len(refs) - 2], refs[-2:]
    me = me_ref[0]

    def piece(which):
        return jnp.concatenate(
            [
                ins[at][:, spec[at][which][0] : spec[at][which][0] + spec[at][which][1]]
                for at in range(n_in)
                if spec[at][which] is not None
            ],
            axis=0,
        )

    def place(chunk, row, cols, block):
        position = lax.bitwise_xor(jnp.int32(chunk), me)
        index = jnp.int32(0)
        for rank, bit in enumerate(order[1:]):
            index = index + lax.bitwise_and(lax.shift_right_logical(position, bit), 1) * (
                2 ** (len(order) - 2 - rank)
            )
        away = lax.bitwise_and(lax.shift_right_logical(position, order[0]), 1)
        rows = slice(row, row + block.shape[0])

        @pl.when(away == 1)
        def send_it():
            sent[index, rows, cols] = block

        @pl.when(away == 0)
        def keep_it():
            kept[index, rows, cols] = block

    left = piece("left")
    chunk_rows = left.shape[1] // n_dp
    for at_piece in range(pieces):
        right = piece("right") if pieces == 1 else piece("right%d" % at_piece)
        columns = right.shape[1]
        tile = 512 if columns % 512 == 0 else columns
        for at in range(0, columns, tile):
            product = tn(left, right[:, at : at + tile]).astype(BF16)
            for chunk in range(n_dp):
                place(
                    chunk,
                    at_piece * chunk_rows,
                    slice(at, at + tile),
                    product[chunk * chunk_rows : (chunk + 1) * chunk_rows],
                )
    if extra:
        for chunk in range(n_dp):
            place(chunk, pieces * chunk_rows, slice(None), tail[0][chunk].astype(BF16))


def weight_kernel(name, n_dp, order, me, spec, arrays, columns, pieces=1, tail=None):
    chunk_rows = 768 // n_dp
    model = max(s["left"][0] + s["left"][1] for s in spec if s["left"] is not None)
    first = next(s["left"] for s in spec if s["left"] is not None)
    chunk_rows = first[1] // n_dp
    rows = pieces * chunk_rows + (0 if tail is None else tail.shape[1])
    shape = (n_dp // 2, rows, columns)
    extra = tail is not None
    body = functools.partial(weight_body, n_dp, order, pieces, extra, spec)
    return call(body, [(shape, BF16), (shape, BF16)], name, 1, len(spec) + int(extra))(
        me, *arrays, *((tail,) if extra else ())
    )


def swap_cores(value):
    return lax.ppermute(value, "tensor", [(0, 1), (1, 0)])


def scatter_sum(order, n_dp, sent, kept):
    for rank, bit in enumerate(order):
        received = lax.ppermute(sent, "dp", [(i, i ^ (1 << bit)) for i in range(n_dp)])
        total = kept.astype(F32) + received.astype(F32)
        if rank == len(order) - 1:
            return total[0]
        half = total.shape[0] // 2
        kept, sent = total[:half].astype(BF16), total[half:].astype(BF16)


def body(
    images, cotangent, live_images, attn_norm_gain, attn_norm_bias, qkv_weight, qv_bias,
    out_weight, out_bias, mlp_norm_gain, mlp_norm_bias, up_weight, up_bias, down_weight, down_bias,
):
    sections = lax.axis_size("section")
    n_dp = lax.axis_size("dp")
    cores = lax.axis_size("tensor")
    section = lax.axis_index("section")
    tensor = lax.axis_index("tensor")
    me = lax.axis_index("dp").astype(jnp.int32).reshape(1)
    row_count, model = images.shape
    slots = row_count // SEQ
    mine = slots // cores
    wqkv, wo, wup, wdown = qkv_weight[0], out_weight[0], up_weight[0], down_weight[0]
    width, hidden = wo.shape[0], wup.shape[1]
    up_bias_row = up_bias
    bits = n_dp.bit_length() - 1

    wqkv_o = swap_cores(wqkv)
    wo_o = swap_cores(wo)
    wup_o = swap_cores(wup)
    wdown_o = swap_cores(wdown)
    qvb, qvb_o = qv_bias[0], swap_cores(qv_bias[0])
    ub, ub_o = up_bias, swap_cores(up_bias)

    flags = jnp.stack([section.astype(jnp.int32), jnp.int32(sections)])
    live = (jnp.arange(slots, dtype=jnp.int32) < live_images[0]).astype(F32)
    masks = lax.dynamic_slice_in_dim(live, tensor * mine, mine).reshape(mine, 1)

    def padded(rows):
        own = lax.dynamic_index_in_dim(rows.reshape(cores, mine, SEQ, model), tensor, 0, keepdims=False)
        return jnp.pad(own, ((0, 0), (0, ROWS - SEQ), (0, 0)))

    image_blocks = padded(images)
    cot_blocks = padded(cotangent)

    fwd_attn = call(
        fwd_attn_body,
        [((ROWS, model), F32), ((ROWS, model), BF16), ((ROWS, model + width), BF16),
         ((ROWS, width), BF16), ((2, 3, ROWS, width), BF16),
         ((2, width // HEAD_DIM, ROWS, ROWS), BF16)],
        "fwd_attn", 1, 11,
    )
    fwd_mlp = call(
        fwd_mlp_body,
        [((ROWS, model), BF16), ((ROWS, model + hidden), BF16), ((ROWS, hidden), BF16),
         ((2, ROWS, hidden), BF16)],
        "fwd_mlp", 1, 10,
    )
    bwd_mlp = call(
        bwd_mlp_body,
        [((ROWS, model), F32), ((ROWS, model), BF16), ((ROWS, model + hidden), BF16),
         ((ROWS, hidden), BF16), ((4, model), F32), ((2, hidden), F32)],
        "bwd_mlp", 2, 9,
    )
    bwd_attn = call(
        bwd_attn_body,
        [((ROWS, model), BF16), ((ROWS, 3 * width), BF16), ((ROWS, 3 * width), BF16),
         ((2, model), F32), ((4, width), F32)],
        "bwd_attn", 0, 9,
    )

    def forward(own, arrived, mask):
        resid, entered, pack_a, ctx, qkv_s, probs_s = fwd_attn(
            flags, own, arrived, attn_norm_gain, attn_norm_bias, wqkv, wqkv_o, qvb, qvb_o, wo, wo_o,
            out_bias,
        )
        leaving, pack_m, act, slope_s = fwd_mlp(
            mask, resid, mlp_norm_gain, mlp_norm_bias, wup, wup_o, ub, ub_o, wdown, wdown_o, down_bias
        )
        return leaving, (resid, entered, pack_a, ctx, qkv_s, probs_s, pack_m, act, slope_s)

    def backward(own, arrived, mask, kept):
        resid, entered, pack_a, ctx, qkv_s, probs_s, pack_m, act, slope_s = kept
        grad_res, gout, pack_g, gup, small_m, bias_u = bwd_mlp(
            flags, mask, own, arrived, resid, slope_s, mlp_norm_gain, wup, wup_o, wdown, wdown_o
        )
        leaving, gqkv, pack_q, small_a, bias_q = bwd_attn(
            grad_res, entered, qkv_s, probs_s, attn_norm_gain, wqkv, wqkv_o, wo, wo_o
        )
        return leaving, (gout, pack_g, gup, gqkv, pack_q, small_m, small_a, bias_u, bias_q)

    onward = [(i, i + 1) for i in range(sections - 1)]
    arrived = [image_blocks[i] for i in range(mine)]
    for step in range(sections):
        results = []
        for i in range(mine):
            leaving, kept = forward(image_blocks[i], arrived[i], masks[i])
            results.append((leaving, kept))
            if step < sections - 1:
                arrived[i] = lax.ppermute(leaving, "section", onward)
    outs = [leaving for leaving, kept in results]
    stored = [kept for leaving, kept in results]

    def for_partner(kept):
        return swap_cores(kept[2]), swap_cores(kept[6])

    partner_fwd = [for_partner(kept) for kept in stored]

    back = [(i + 1, i) for i in range(sections - 1)]
    arrived = [cot_blocks[i] for i in range(mine)]
    for step in range(sections):
        results = []
        for i in range(mine):
            leaving, grads = backward(cot_blocks[i], arrived[i], masks[i], stored[i])
            results.append((leaving, grads))
            if step < sections - 1:
                arrived[i] = lax.ppermute(leaving, "section", back)
    grads_in = [leaving for leaving, grads in results]
    grads = [g for leaving, g in results]

    p_gout = [swap_cores(g[0]) for g in grads]
    p_pack_g = [swap_cores(g[1]) for g in grads]
    p_pack_q = [swap_cores(g[4]) for g in grads]

    order_a = tuple(range(bits))
    order_b = (1, 0) + tuple(range(2, bits)) if bits > 1 else order_a

    full = (0, model)

    def both(left, right):
        return {"left": left, "right": right}

    arrays, spec = [], []
    for i in range(mine):
        arrays += [grads[i][0], stored[i][7]]
        spec += [both(full, None), both(None, (0, hidden))]
    for i in range(mine):
        arrays += [p_gout[i], partner_fwd[i][1]]
        spec += [both(full, None), both(None, (model, hidden))]
    down_sum = scatter_sum(order_a, n_dp, *weight_kernel("w_down", n_dp, order_a, me, spec, arrays, hidden))

    arrays, spec = [], []
    for i in range(mine):
        arrays += [stored[i][6], grads[i][2]]
        spec += [both(full, None), both(None, (0, hidden))]
    for i in range(mine):
        arrays += [partner_fwd[i][1], p_pack_g[i]]
        spec += [both(full, None), both(None, (model, hidden))]
    up_sum = scatter_sum(order_a, n_dp, *weight_kernel("w_up", n_dp, order_a, me, spec, arrays, hidden))

    arrays, spec = [], []
    for i in range(mine):
        arrays += [grads[i][1], stored[i][3]]
        spec += [both(full, None), both(None, (0, width))]
    for i in range(mine):
        arrays += [p_pack_g[i], partner_fwd[i][0]]
        spec += [both(full, None), both(None, (model, width))]
    out_sum = scatter_sum(order_a, n_dp, *weight_kernel("w_out", n_dp, order_a, me, spec, arrays, width))

    def summed(index):
        total = grads[0][index]
        for g in grads[1:]:
            total = total + g[index]
        return total

    small_m, small_a, bias_u, bias_q = summed(5), summed(6), summed(7), summed(8)
    flat = jnp.concatenate([small_a.reshape(-1), small_m.reshape(-1), bias_u[1], bias_q[2:4].reshape(-1)])
    flat_p = swap_cores(flat)
    own_flat = jnp.concatenate([small_a.reshape(-1), small_m.reshape(-1), bias_u[0], bias_q[0:2].reshape(-1)])
    flat = own_flat + flat_p
    part = model // n_dp
    six = flat[: 6 * model].reshape(6, n_dp, part)
    bu = flat[6 * model : 6 * model + hidden].reshape(n_dp, hidden // n_dp)
    bq = flat[6 * model + hidden :].reshape(2, n_dp, width // n_dp)
    tail = jnp.concatenate(
        [six.transpose(1, 0, 2).reshape(n_dp, -1), bu, bq.transpose(1, 0, 2).reshape(n_dp, -1)], axis=1
    )
    used = tail.shape[1]
    tail_rows = -(-used // (16 * width)) * 16
    tail = jnp.pad(tail, ((0, 0), (0, tail_rows * width - used))).reshape(n_dp, tail_rows, width)

    arrays, spec = [], []
    for i in range(mine):
        arrays += [stored[i][2], grads[i][3]]
        spec += [{"left": full, "right0": None, "right1": None, "right2": None},
                 {"left": None, **{"right%d" % j: (j * width, width) for j in range(3)}}]
    for i in range(mine):
        arrays += [partner_fwd[i][0], p_pack_q[i]]
        spec += [{"left": full, "right0": None, "right1": None, "right2": None},
                 {"left": None, **{"right%d" % j: (j * width, width) for j in range(3)}}]
    qkv_sum = scatter_sum(
        order_b, n_dp,
        *weight_kernel("w_qkv", n_dp, order_b, me, spec, arrays, width, pieces=3, tail=tail),
    )

    small = qkv_sum[3 * part :].reshape(-1)[:used]
    g_small = small[: 6 * part].reshape(6, 1, part)
    g_bu = small[6 * part : 6 * part + hidden // n_dp].reshape(1, -1)
    g_bq = small[6 * part + hidden // n_dp :].reshape(1, 2, -1)

    def whole(blocks):
        own = jnp.stack([b[:SEQ] for b in blocks]).reshape(mine * SEQ, model)
        other = swap_cores(jnp.stack(blocks))[:, :SEQ].reshape(mine * SEQ, model)
        first = jnp.where(tensor == 0, own, other)
        second = jnp.where(tensor == 0, other, own)
        return jnp.concatenate([first, second], axis=0)[None]

    return (
        whole(outs),
        whole(grads_in),
        g_small[0],
        g_small[1],
        qkv_sum[: 3 * part].reshape(1, 3, part, width),
        g_bq,
        out_sum.T[None],
        g_small[2],
        g_small[3],
        g_small[4],
        up_sum[None],
        g_bu,
        down_sum.T[None],
        g_small[5],
    )


def solution(mesh):
    in_specs = (
        P("dp", None), P("dp", None), P("dp"),
        P("section", None), P("section", None),
        P("section", None, None, "tensor"), P("section", None, "tensor"),
        P("section", "tensor", None), P("section", None),
        P("section", None), P("section", None),
        P("section", None, "tensor"), P("section", "tensor"),
        P("section", "tensor", None), P("section", None),
    )
    out_specs = (
        P("section", "dp", None), P("section", "dp", None),
        P("section", "dp"), P("section", "dp"),
        P("section", None, "dp", "tensor"), P("section", None, ("tensor", "dp")),
        P("section", "tensor", "dp"), P("section", "dp"),
        P("section", "dp"), P("section", "dp"),
        P("section", "dp", "tensor"), P("section", ("tensor", "dp")),
        P("section", "tensor", "dp"), P("section", "dp"),
    )
    return jax.shard_map(body, mesh=mesh, in_specs=in_specs, out_specs=out_specs, check_vma=False)
```
